32 devices in a mesh: pipe: 4 (over x, core), dp: 8 (over z, y).
Axes of the slice: x: 2, y: 2, z: 4, core: 2. Of those that a mesh axis runs over, the one named last changes fastest.
Arguments:
- section_input: bfloat16 [4, 2048, 2048], P('pipe', 'dp'), may hold values from -6 to 6
- top_grad: bfloat16 [2048, 2048], P('dp'), may hold values from -6 to 6
- w_in: bfloat16 [4, 2048, 3072], P('pipe', 'dp'), may hold values from -0.125 to 0.125
- w_out: bfloat16 [4, 1024, 2048], P('pipe', 'dp'), may hold values from -0.1875 to 0.1875
- segments: int32 [16, 128], P('dp'), may hold values from 0 to 3, never falling along the last dimension, each value on 1 to 64 neighbouring positions
Outputs:
- section_grads: bfloat16 [4, 2048, 2048], P('pipe', 'dp')
- w_in_grad: float32 [4, 2048, 3072], P('pipe', 'dp')
- w_out_grad: float32 [4, 1024, 2048], P('pipe', 'dp')
The draws below stay inside these ranges and needn't reach their ends.
Inputs may be any that keep to these rules, and one draw needn't show every extreme that they name: `segments`: in every row the history numbers run 0 to 3 without falling, each history has 1 to 64 positions, and one has exactly 64.
All inputs are finite; a program needn't handle non-finite values.
Results may differ from the reference program's by a relative error of at most 0.03.
Values may be sent and summed in bfloat16 or wider, within the bound.
A program may use at most 128 MiB of HBM per device.

```python
import math
import jax
import jax.numpy as jnp
import numpy as np
from jax import lax

D = 2048
HEADS = 16
QK_DIM = 32
V_DIM = 64
HV = 1024
F1 = 3072
TOK_MB = 128
MICRO = 2
SEGS = 4
SEG_MOST = 64
SECTIONS = 4
TOKENS = 2048
MB_ROWS = 16
N_PIPE = 4
N_DP = 8


def spiked(array, own_key, source, target, shards_of, factor):
    owner, partner = [(jnp.arange(array.shape[dim]) // (array.shape[dim] // shards_of)).reshape([-1 if axis == dim else 1 for axis in range(array.ndim)]) for dim in (source, target)]
    chosen = jax.random.permutation(own_key, shards_of)[partner]
    strong = (owner == chosen) | (owner == (partner + shards_of // 2) % shards_of)
    return jnp.where(strong, factor * array, array)


def levels(rng, dims, split, smallest, largest):
    def one(dim, shards_of):
        heights = jax.random.uniform(jax.random.fold_in(jax.random.fold_in(rng, 6), dim), (shards_of,), jnp.float32, smallest / len(split), largest / len(split))
        return jnp.repeat(jnp.exp(heights), dims[dim] // shards_of).reshape((-1,) + (1,) * (len(dims) - dim - 1))

    loudness = one(*split[0])
    for cut in split[1:]:
        loudness = loudness * one(*cut)
    return loudness


def profile(count, total, reach, skew):
    loads = [(1 << 20) // math.isqrt(standing ** skew) + 1 for standing in range(2, count + 1)]
    spare, given = total - reach - (count - 1), [1] * (count - 1)
    while spare > 0:
        free = [i for i in range(count - 1) if given[i] < reach]
        mass, left = sum([loads[i] for i in free]), spare
        for i in free:
            extra = min(reach - given[i], max(1, left * loads[i] // mass), spare)
            given[i] = given[i] + extra
            spare = spare - extra
    return np.array([reach] + given)


def ragged_sizes(stream_key, amount, total, bound, lean):
    if amount == 2:
        one = jax.random.randint(stream_key, (), max(1, total - bound), min(bound, total - 1) + 1)
        return jnp.stack([one, total - one])
    tallies = jnp.asarray(profile(amount, total, bound, lean), jnp.int32)
    twos = (amount - 1) // 2
    giver, receiver = tallies[1:1 + 2 * twos:2], tallies[2:2 + 2 * twos:2]
    room = jnp.minimum(giver - 1, bound - receiver)
    moved = jax.random.randint(jax.random.fold_in(stream_key, 1), (twos,), 0, 1 << 20) % (room + 1)
    tallies = tallies.at[1:1 + 2 * twos:2].set(giver - moved).at[2:2 + 2 * twos:2].set(receiver + moved)
    return tallies[jax.random.permutation(jax.random.fold_in(stream_key, 2), amount)]


def gaussian(rng, dims, width, most, cuts=(), kind=jnp.bfloat16):
    gain = levels(rng, dims, cuts, -0.22, 0.18) if cuts else 1.0
    array = jax.random.normal(rng, dims, jnp.float32) * width * gain
    return jnp.minimum(jnp.maximum(array, -most), most).astype(kind)


def heavy_noise(own_key, shape, spread, reach, cuts, heavy, kind=jnp.bfloat16):
    values = spread * jax.random.normal(own_key, shape, jnp.float32)
    if cuts:
        values = values * levels(own_key, shape, cuts, -0.22, 0.18)
    return jnp.clip(spiked(values, jax.random.fold_in(own_key, 3), *heavy), -reach, reach).astype(kind)


def setup_inputs(seed: int = 0) -> dict:
    seeds = jax.random.split(jax.random.key(seed), 6)
    section_input = heavy_noise(seeds[0], (SECTIONS, TOKENS, D), 1.0, 6.0, ((0, 4), (1, 8)), (1, 2, 8, 2.0))
    top_grad = gaussian(seeds[1], (TOKENS, D), 1.0, 6.0, ((0, 8),))
    w_in = gaussian(seeds[2], (SECTIONS, D, F1), D ** -0.5, 0.125, ((0, 4), (1, 8)))
    w_out = gaussian(seeds[3], (SECTIONS, HV, D), HV ** -0.5, 0.1875, ((0, 4), (1, 8)))
    segments = jax.vmap(lambda own: jnp.searchsorted(jnp.cumsum(ragged_sizes(own, SEGS, TOK_MB, SEG_MOST, 2)), jnp.arange(TOK_MB), side="right"))(jax.random.split(seeds[4], MB_ROWS)).reshape((MB_ROWS, TOK_MB)).astype(jnp.int32)
    return {"section_input": section_input, "top_grad": top_grad, "w_in": w_in, "w_out": w_out, "segments": segments}


EPSILON = 1e-05

def norm_rows(values):
    center = values - lax.optimization_barrier(jnp.mean(values, axis=-1, keepdims=True))
    return center * lax.rsqrt(lax.optimization_barrier(jnp.mean(center * center, axis=-1, keepdims=True)) + EPSILON)

def silu_slope(preact):
    squash = jax.nn.sigmoid(preact)
    return squash * (1.0 + preact * (1.0 - squash))

def contract_rows(left, right):
    return lax.dot_general(left, right, (((0,), (0,)), ((), ())), preferred_element_type=jnp.float32)

def forward_front(inputs, w_first):
    normed = norm_rows(inputs.astype(jnp.float32)).astype(jnp.bfloat16)
    preact = jnp.dot(normed, w_first, preferred_element_type=jnp.float32)
    return (normed, preact, jax.nn.silu(preact).astype(jnp.bfloat16))

def attend(activated, history):
    row_count = activated.shape[0]
    value_cols = HEADS * V_DIM
    query_cols = HEADS * QK_DIM
    active32 = activated.astype(jnp.float32)
    gating = active32[:, :value_cols]
    values = active32[:, value_cols:2 * value_cols].reshape(row_count, HEADS, V_DIM)
    queries = active32[:, 2 * value_cols:2 * value_cols + query_cols].reshape(row_count, HEADS, QK_DIM)
    key_rows = active32[:, 2 * value_cols + query_cols:].reshape(row_count, HEADS, QK_DIM)
    scores = jnp.einsum('qhd,khd->hqk', queries, key_rows) * QK_DIM ** (-0.5)
    same_doc = history[:, None] == history[None, :]
    positions = lax.broadcasted_iota(jnp.int32, (row_count, row_count), 0)
    columns = lax.broadcasted_iota(jnp.int32, (row_count, row_count), 1)
    allowed = jnp.logical_and(same_doc, columns <= positions)
    counts = lax.optimization_barrier(jnp.sum(same_doc.astype(jnp.float32), axis=1))
    weights_mask = allowed.astype(jnp.float32) / counts[:, None]
    weights = jax.nn.silu(scores) * weights_mask[None]
    mixed = jnp.einsum('hqk,khd->qhd', weights, values).reshape(row_count, value_cols)
    return norm_rows(mixed) * gating

def layer_back(inputs, normed, preact, activated, upstream, history, w_first, w_second):
    gated_full, pull = jax.vjp(lambda active_in: attend(active_in, history), activated)
    gated = gated_full.astype(jnp.bfloat16)
    grad_second = contract_rows(gated, upstream)
    grad_gated = lax.dot_general(upstream, w_second, (((1,), (1,)), ((), ())), preferred_element_type=jnp.float32)
    grad_active, = pull(grad_gated)
    grad_preact = (grad_active.astype(jnp.float32) * silu_slope(preact)).astype(jnp.bfloat16)
    grad_normed = lax.dot_general(grad_preact, w_first, (((1,), (1,)), ((), ())), preferred_element_type=jnp.float32)
    _, pull_norm = jax.vjp(norm_rows, inputs.astype(jnp.float32))
    grad_through, = pull_norm(grad_normed)
    grad_input = (upstream.astype(jnp.float32) + grad_through).astype(jnp.bfloat16)
    return (grad_input, grad_preact, grad_second)

def reference(section_input, top_grad, w_in, w_out, segments):
    upstream_all = top_grad
    section_list = []
    first_list = []
    second_list = []
    for section in range(N_PIPE - 1, -1, -1):
        inputs_all = section_input[section]
        w_first = w_in[section]
        w_second = w_out[section]
        upstream_now = upstream_all

        def device_step(carry, device):
            total_in, total_out = carry
            acc_in = jnp.zeros((D, F1), jnp.float32)
            acc_out = jnp.zeros((HV, D), jnp.float32)
            pieces = []
            for micro_index in range(MICRO):
                block = (device * MICRO + micro_index).astype(jnp.int32)
                start = (block * TOK_MB).astype(jnp.int32)
                inputs = lax.dynamic_slice_in_dim(inputs_all, start, TOK_MB, 0)
                upstream = lax.dynamic_slice_in_dim(upstream_now, start, TOK_MB, 0)
                history = lax.dynamic_index_in_dim(segments, block, 0, keepdims=False)
                normed, preact, activated = forward_front(inputs, w_first)
                grad_input, grad_preact, grad_second = layer_back(inputs, normed, preact, activated, upstream, history, w_first, w_second)
                acc_in = acc_in + contract_rows(normed, grad_preact)
                acc_out = acc_out + grad_second
                pieces.append(grad_input)
            total_in = total_in + lax.optimization_barrier(acc_in.astype(jnp.bfloat16)).astype(jnp.float32)
            total_out = total_out + lax.optimization_barrier(acc_out.astype(jnp.bfloat16)).astype(jnp.float32)
            return ((total_in, total_out), jnp.concatenate(pieces, axis=0))
        start_sums = (jnp.zeros((D, F1), jnp.float32), jnp.zeros((HV, D), jnp.float32))
        (total_in, total_out), grad_blocks = lax.scan(device_step, start_sums, jnp.arange(N_DP, dtype=jnp.int32))
        upstream_all = grad_blocks.reshape(TOKENS, D)
        section_list.insert(0, upstream_all)
        first_list.insert(0, total_in)
        second_list.insert(0, total_out)
    return (jnp.stack(section_list), jnp.stack(first_list), jnp.stack(second_list))
```

```python
import functools

import jax
import jax.numpy as jnp
from jax import lax
from jax.experimental import pallas as pl
from jax.experimental.pallas import tpu as pltpu
from jax.sharding import PartitionSpec as P

HEADS = 16
QK_DIM = 32
V_DIM = 64
LANES = 128

EPSILON = 1e-05
MESH = pl.DeviceIdType.MESH
VMEM = pl.BlockSpec(memory_space=pltpu.VMEM)

QK_HEADS = LANES // QK_DIM
V_HEADS = LANES // V_DIM
GROUPS = HEADS // QK_HEADS
V_COLS = HEADS * V_DIM
Q_COLS = HEADS * QK_DIM
GROUP_V = QK_HEADS * V_DIM
SCALE = QK_DIM ** (-0.5)


def norm_rows(values):
    center = values - jnp.mean(values, axis=-1, keepdims=True)
    return center * lax.rsqrt(jnp.mean(center * center, axis=-1, keepdims=True) + EPSILON)


def silu_slope(preact):
    squash = jax.nn.sigmoid(preact)
    return squash * (1.0 + preact * (1.0 - squash))


def dot_nt(left, right):
    return lax.dot_general(
        left, right, (((1,), (1,)), ((), ())), preferred_element_type=jnp.float32
    )


def dot_nn(left, right):
    return lax.dot_general(
        left, right, (((1,), (0,)), ((), ())), preferred_element_type=jnp.float32
    )


def contract_rows(left, right):
    return lax.dot_general(
        left, right, (((0,), (0,)), ((), ())), preferred_element_type=jnp.float32
    )


def only_head(block, lane, width, index):
    keep = jnp.logical_and(lane >= index * width, lane < (index + 1) * width)
    return jnp.where(keep, block, jnp.zeros_like(block))


def at(start, size):
    return pl.ds(pl.multiple_of(start, LANES), size)


def attend_kernel(micro, length, act_ref, mask_ref, score_ref, unit_ref, rstd_ref, gated_ref, mixed):
    lane = lax.broadcasted_iota(jnp.int32, (length, LANES), 1)

    def one(index, _):
        slot, group = index // GROUPS, index % GROUPS
        rows = at(slot * length, length)
        queries = act_ref[rows, at(2 * V_COLS + group * LANES, LANES)]
        keys = act_ref[rows, at(2 * V_COLS + Q_COLS + group * LANES, LANES)]
        mask = mask_ref[rows, :]
        for half in range(GROUP_V // LANES):
            cols = group * GROUP_V + half * LANES
            values = act_ref[rows, at(V_COLS + cols, LANES)]
            total = jnp.zeros((length, LANES), jnp.float32)
            for sub in range(V_HEADS):
                head = half * V_HEADS + sub
                score = dot_nt(only_head(queries, lane, QK_DIM, head), keys) * SCALE
                score_ref[at((index * QK_HEADS + head) * length, length), :] = score
                weight = (jax.nn.silu(score) * mask).astype(jnp.bfloat16)
                total += dot_nn(weight, only_head(values, lane, V_DIM, sub))
            mixed[rows, at(cols, LANES)] = total
        return 0

    lax.fori_loop(0, micro * GROUPS, one, 0)

    def finish(slot, _):
        rows = at(slot * length, length)
        value = mixed[rows, :]
        center = value - jnp.mean(value, axis=-1, keepdims=True)
        rstd = lax.rsqrt(jnp.mean(center * center, axis=-1, keepdims=True) + EPSILON)
        unit = center * rstd
        unit_ref[rows, :] = unit
        rstd_ref[rows, :] = jnp.broadcast_to(rstd, (length, LANES))
        gated_ref[rows, :] = (unit * act_ref[rows, :V_COLS].astype(jnp.float32)).astype(jnp.bfloat16)
        return 0

    lax.fori_loop(0, micro, finish, 0)


def attend(activated, mask, micro, length):
    tokens = micro * length
    return pl.pallas_call(
        functools.partial(attend_kernel, micro, length),
        out_shape=(
            jax.ShapeDtypeStruct((micro * HEADS * length, length), jnp.float32),
            jax.ShapeDtypeStruct((tokens, V_COLS), jnp.float32),
            jax.ShapeDtypeStruct((tokens, LANES), jnp.float32),
            jax.ShapeDtypeStruct((tokens, V_COLS), jnp.bfloat16),
        ),
        in_specs=[VMEM] * 2,
        out_specs=(VMEM,) * 4,
        scratch_shapes=[pltpu.VMEM((tokens, V_COLS), jnp.float32)],
        name="attend",
    )(activated, mask)


def chain_kernel(
    micro, length, sections,
    top_ref, input_ref, act_ref, pre_ref, score_ref, unit_ref, rstd_ref, mask_ref, first_ref, second_ref,
    up_ref, gpre_ref, gin_ref,
    landed, leaving, ggate, dmix, gnorm, send_sem, recv_sem,
):
    section = lax.axis_index("pipe")
    width = input_ref.shape[1]
    tile = 2 * LANES
    lane = lax.broadcasted_iota(jnp.int32, (length, LANES), 1)
    is_last = section == sections - 1
    is_first = section == 0

    barrier = pltpu.get_barrier_semaphore()

    @pl.when(jnp.logical_not(is_last))
    def _():
        pl.semaphore_signal(
            barrier, inc=1, device_id={"pipe": jnp.minimum(section + 1, sections - 1)}, device_id_type=MESH
        )

    @pl.when(jnp.logical_not(is_first))
    def _():
        pl.semaphore_wait(barrier, 1)

    def copy_of(slot):
        return pltpu.make_async_remote_copy(
            src_ref=leaving.at[slot],
            dst_ref=landed.at[slot],
            send_sem=send_sem.at[slot],
            recv_sem=recv_sem.at[slot],
            device_id={"pipe": jnp.maximum(section - 1, 0)},
            device_id_type=MESH,
        )

    def store_grad(rows, cols, size, value):
        rounded = value.astype(jnp.bfloat16).astype(jnp.float32)
        gpre_ref[rows, at(cols, size)] = (
            rounded * silu_slope(pre_ref[rows, at(cols, size)])
        ).astype(jnp.bfloat16)

    for slot in range(micro):
        rows = pl.ds(slot * length, length)

        @pl.when(is_last)
        def _():
            up_ref[rows, :] = top_ref[rows, :]

        @pl.when(jnp.logical_not(is_last))
        def _():
            copy_of(slot).wait_recv()
            up_ref[rows, :] = landed[slot]

        def gate_tile(index, _):
            ggate[:, at(index * tile, tile)] = dot_nt(up_ref[rows, :], second_ref[at(index * tile, tile), :])
            return 0

        lax.fori_loop(0, V_COLS // tile, gate_tile, 0)
        gating = act_ref[rows, :V_COLS].astype(jnp.float32)
        unit = unit_ref[rows, :]
        grad = ggate[...]
        store_grad(rows, 0, V_COLS, grad * unit)
        grad = grad * gating
        mean_grad = jnp.mean(grad, axis=-1, keepdims=True)
        mean_unit = jnp.mean(grad * unit, axis=-1, keepdims=True)
        dmix[...] = (rstd_ref[rows, :1] * (grad - mean_grad - unit * mean_unit)).astype(jnp.bfloat16)

        def one(group, _):
            queries = act_ref[rows, at(2 * V_COLS + group * LANES, LANES)]
            keys = act_ref[rows, at(2 * V_COLS + Q_COLS + group * LANES, LANES)]
            mask = mask_ref[rows, :]
            grad_q = jnp.zeros((length, LANES), jnp.float32)
            grad_k = jnp.zeros((length, LANES), jnp.float32)
            for half in range(GROUP_V // LANES):
                cols = group * GROUP_V + half * LANES
                values = act_ref[rows, at(V_COLS + cols, LANES)]
                grad_mix = dmix[:, at(cols, LANES)]
                grad_v = jnp.zeros((length, LANES), jnp.float32)
                for sub in range(V_HEADS):
                    head = half * V_HEADS + sub
                    mix_head = only_head(grad_mix, lane, V_DIM, sub)
                    place = (slot * HEADS + group * QK_HEADS + head) * length
                    score = score_ref[at(place, length), :]
                    squash = jax.nn.sigmoid(score)
                    weight = (score * squash * mask).astype(jnp.bfloat16)
                    slope = squash * (1.0 + score * (1.0 - squash)) * mask * SCALE
                    grad_score = (dot_nt(mix_head, values) * slope).astype(jnp.bfloat16)
                    grad_v += contract_rows(weight, mix_head)
                    grad_q += dot_nn(grad_score, only_head(keys, lane, QK_DIM, head))
                    grad_k += contract_rows(grad_score, only_head(queries, lane, QK_DIM, head))
                store_grad(rows, V_COLS + cols, LANES, grad_v)
            store_grad(rows, 2 * V_COLS + group * LANES, LANES, grad_q)
            store_grad(rows, 2 * V_COLS + Q_COLS + group * LANES, LANES, grad_k)
            return 0

        lax.fori_loop(0, GROUPS, one, 0)

        def norm_tile(index, _):
            gnorm[:, at(index * tile, tile)] = dot_nt(gpre_ref[rows, :], first_ref[at(index * tile, tile), :])
            return 0

        lax.fori_loop(0, width // tile, norm_tile, 0)
        value = input_ref[rows, :].astype(jnp.float32)
        center = value - jnp.mean(value, axis=-1, keepdims=True)
        rstd = lax.rsqrt(jnp.mean(center * center, axis=-1, keepdims=True) + EPSILON)
        unit = center * rstd
        grad = gnorm[...]
        mean_grad = jnp.mean(grad, axis=-1, keepdims=True)
        mean_unit = jnp.mean(grad * unit, axis=-1, keepdims=True)
        through = rstd * (grad - mean_grad - unit * mean_unit)
        result = (up_ref[rows, :].astype(jnp.float32) + through).astype(jnp.bfloat16)
        leaving[slot] = result
        gin_ref[rows, :] = result

        @pl.when(jnp.logical_not(is_first))
        def _():
            copy_of(slot).start()

    for slot in range(micro):

        @pl.when(jnp.logical_not(is_first))
        def _():
            copy_of(slot).wait_send()


def chain(top, inputs, activated, preact, scores, unit, rstd, mask, w_first, w_second, micro, length):
    tokens, width = inputs.shape
    return pl.pallas_call(
        functools.partial(chain_kernel, micro, length, lax.axis_size("pipe")),
        out_shape=(
            jax.ShapeDtypeStruct((tokens, width), jnp.bfloat16),
            jax.ShapeDtypeStruct(preact.shape, jnp.bfloat16),
            jax.ShapeDtypeStruct((tokens, width), jnp.bfloat16),
        ),
        in_specs=[VMEM] * 10,
        out_specs=(VMEM,) * 3,
        scratch_shapes=[
            pltpu.VMEM((micro, length, width), jnp.bfloat16),
            pltpu.VMEM((micro, length, width), jnp.bfloat16),
            pltpu.VMEM((length, V_COLS), jnp.float32),
            pltpu.VMEM((length, V_COLS), jnp.bfloat16),
            pltpu.VMEM((length, width), jnp.float32),
            pltpu.SemaphoreType.DMA((micro,)),
            pltpu.SemaphoreType.DMA((micro,)),
        ],
        compiler_params=pltpu.CompilerParams(
            collective_id=0, has_side_effects=True, vmem_limit_bytes=60 * 1024 * 1024
        ),
        name="chain",
    )(top, inputs, activated, preact, scores, unit, rstd, mask, w_first, w_second)


def mask_of(segments):
    length = segments.shape[1]
    same = segments[:, :, None] == segments[:, None, :]
    positions = lax.broadcasted_iota(jnp.int32, (length, length), 0)
    columns = lax.broadcasted_iota(jnp.int32, (length, length), 1)
    counts = jnp.sum(same.astype(jnp.float32), axis=2, keepdims=True)
    allowed = jnp.logical_and(same, (columns <= positions)[None])
    return (allowed.astype(jnp.float32) / counts).reshape(-1, length)


def body(section_input, top_grad, w_in, w_out, segments):
    micro, length = segments.shape
    inputs = section_input[0]
    w_first = lax.all_gather(w_in[0], "dp", axis=0, tiled=True)
    w_mine, w_first = lax.optimization_barrier((w_out[0], w_first))
    w_second = lax.all_gather(w_mine, "dp", axis=0, tiled=True)
    mask = mask_of(segments)
    normed = norm_rows(inputs.astype(jnp.float32)).astype(jnp.bfloat16)
    preact = jnp.dot(normed, w_first, preferred_element_type=jnp.float32)
    activated = jax.nn.silu(preact).astype(jnp.bfloat16)
    scores, unit, rstd, gated = attend(activated, mask, micro, length)
    upstream, grad_preact, grads = chain(
        top_grad, inputs, activated, preact, scores, unit, rstd, mask, w_first, w_second, micro, length
    )
    part_out = contract_rows(gated, upstream).astype(jnp.bfloat16)
    grad_out = lax.psum_scatter(part_out, "dp", scatter_dimension=0, tiled=True).astype(jnp.float32)
    part_in = contract_rows(normed, grad_preact).astype(jnp.bfloat16)
    grad_first = lax.psum_scatter(part_in, "dp", scatter_dimension=0, tiled=True).astype(jnp.float32)
    return (grads[None], grad_first[None], grad_out[None])


def solution(mesh):
    return jax.shard_map(
        body,
        mesh=mesh,
        in_specs=(
            P("pipe", "dp", None),
            P("dp", None),
            P("pipe", "dp", None),
            P("pipe", "dp", None),
            P("dp", None),
        ),
        out_specs=(P("pipe", "dp", None), P("pipe", "dp", None), P("pipe", "dp", None)),
        check_vma=False,
    )
```

```python
import functools

import jax
import jax.numpy as jnp
from jax import lax
from jax.experimental import pallas as pl
from jax.experimental.pallas import tpu as pltpu
from jax.sharding import PartitionSpec as P

HEADS = 16
QK_DIM = 32
V_DIM = 64
LANES = 128

EPSILON = 1e-05
MESH = pl.DeviceIdType.MESH
VMEM = pl.BlockSpec(memory_space=pltpu.VMEM)

QK_HEADS = LANES // QK_DIM
V_HEADS = LANES // V_DIM
GROUPS = HEADS // QK_HEADS
V_COLS = HEADS * V_DIM
Q_COLS = HEADS * QK_DIM
GROUP_V = QK_HEADS * V_DIM
SCALE = QK_DIM ** (-0.5)


def norm_rows(values):
    center = values - jnp.mean(values, axis=-1, keepdims=True)
    return center * lax.rsqrt(jnp.mean(center * center, axis=-1, keepdims=True) + EPSILON)


def silu_slope(preact):
    squash = jax.nn.sigmoid(preact)
    return squash * (1.0 + preact * (1.0 - squash))


def dot_nt(left, right):
    return lax.dot_general(
        left, right, (((1,), (1,)), ((), ())), preferred_element_type=jnp.float32
    )


def dot_nn(left, right):
    return lax.dot_general(
        left, right, (((1,), (0,)), ((), ())), preferred_element_type=jnp.float32
    )


def contract_rows(left, right):
    return lax.dot_general(
        left, right, (((0,), (0,)), ((), ())), preferred_element_type=jnp.float32
    )


def only_head(block, lane, width, index):
    keep = jnp.logical_and(lane >= index * width, lane < (index + 1) * width)
    return jnp.where(keep, block, jnp.zeros_like(block))


def at(start, size):
    return pl.ds(pl.multiple_of(start, LANES), size)


def attend_kernel(micro, length, act_ref, mask_ref, score_ref, unit_ref, rstd_ref, gated_ref, mixed):
    lane = lax.broadcasted_iota(jnp.int32, (length, LANES), 1)

    def one(index, _):
        slot, group = index // GROUPS, index % GROUPS
        rows = at(slot * length, length)
        queries = act_ref[rows, at(2 * V_COLS + group * LANES, LANES)]
        keys = act_ref[rows, at(2 * V_COLS + Q_COLS + group * LANES, LANES)]
        mask = mask_ref[rows, :]
        for half in range(GROUP_V // LANES):
            cols = group * GROUP_V + half * LANES
            values = act_ref[rows, at(V_COLS + cols, LANES)]
            total = jnp.zeros((length, LANES), jnp.float32)
            for sub in range(V_HEADS):
                head = half * V_HEADS + sub
                score = dot_nt(only_head(queries, lane, QK_DIM, head), keys) * SCALE
                score_ref[at((index * QK_HEADS + head) * length, length), :] = score
                weight = (jax.nn.silu(score) * mask).astype(jnp.bfloat16)
                total += dot_nn(weight, only_head(values, lane, V_DIM, sub))
            mixed[rows, at(cols, LANES)] = total
        return 0

    lax.fori_loop(0, micro * GROUPS, one, 0)

    def finish(slot, _):
        rows = at(slot * length, length)
        value = mixed[rows, :]
        center = value - jnp.mean(value, axis=-1, keepdims=True)
        rstd = lax.rsqrt(jnp.mean(center * center, axis=-1, keepdims=True) + EPSILON)
        unit = center * rstd
        unit_ref[rows, :] = unit
        rstd_ref[rows, :] = jnp.broadcast_to(rstd, (length, LANES))
        gated_ref[rows, :] = (unit * act_ref[rows, :V_COLS].astype(jnp.float32)).astype(jnp.bfloat16)
        return 0

    lax.fori_loop(0, micro, finish, 0)


def attend(activated, mask, micro, length):
    tokens = micro * length
    return pl.pallas_call(
        functools.partial(attend_kernel, micro, length),
        out_shape=(
            jax.ShapeDtypeStruct((micro * HEADS * length, length), jnp.float32),
            jax.ShapeDtypeStruct((tokens, V_COLS), jnp.float32),
            jax.ShapeDtypeStruct((tokens, LANES), jnp.float32),
            jax.ShapeDtypeStruct((tokens, V_COLS), jnp.bfloat16),
        ),
        in_specs=[VMEM] * 2,
        out_specs=(VMEM,) * 4,
        scratch_shapes=[pltpu.VMEM((tokens, V_COLS), jnp.float32)],
        name="attend",
    )(activated, mask)


def chain_kernel(
    micro, length, sections,
    top_ref, input_ref, act_ref, pre_ref, score_ref, unit_ref, rstd_ref, mask_ref, first_ref, second_ref,
    up_ref, gpre_ref, gin_ref,
    landed, leaving, ggate, dmix, gnorm, send_sem, recv_sem,
):
    section = lax.axis_index("pipe")
    width = input_ref.shape[1]
    tile = 2 * LANES
    lane = lax.broadcasted_iota(jnp.int32, (length, LANES), 1)
    is_last = section == sections - 1
    is_first = section == 0

    barrier = pltpu.get_barrier_semaphore()

    @pl.when(jnp.logical_not(is_last))
    def _():
        pl.semaphore_signal(
            barrier, inc=1, device_id={"pipe": jnp.minimum(section + 1, sections - 1)}, device_id_type=MESH
        )

    @pl.when(jnp.logical_not(is_first))
    def _():
        pl.semaphore_wait(barrier, 1)

    def copy_of(slot):
        return pltpu.make_async_remote_copy(
            src_ref=leaving.at[slot],
            dst_ref=landed.at[slot],
            send_sem=send_sem.at[slot],
            recv_sem=recv_sem.at[slot],
            device_id={"pipe": jnp.maximum(section - 1, 0)},
            device_id_type=MESH,
        )

    def store_grad(rows, cols, size, value):
        rounded = value.astype(jnp.bfloat16).astype(jnp.float32)
        gpre_ref[rows, at(cols, size)] = (
            rounded * silu_slope(pre_ref[rows, at(cols, size)])
        ).astype(jnp.bfloat16)

    for slot in range(micro):
        rows = pl.ds(slot * length, length)

        @pl.when(is_last)
        def _():
            up_ref[rows, :] = top_ref[rows, :]

        @pl.when(jnp.logical_not(is_last))
        def _():
            copy_of(slot).wait_recv()
            up_ref[rows, :] = landed[slot]

        def gate_tile(index, _):
            ggate[:, at(index * tile, tile)] = dot_nt(up_ref[rows, :], second_ref[at(index * tile, tile), :])
            return 0

        lax.fori_loop(0, V_COLS // tile, gate_tile, 0)
        gating = act_ref[rows, :V_COLS].astype(jnp.float32)
        unit = unit_ref[rows, :]
        grad = ggate[...]
        store_grad(rows, 0, V_COLS, grad * unit)
        grad = grad * gating
        mean_grad = jnp.mean(grad, axis=-1, keepdims=True)
        mean_unit = jnp.mean(grad * unit, axis=-1, keepdims=True)
        dmix[...] = (rstd_ref[rows, :1] * (grad - mean_grad - unit * mean_unit)).astype(jnp.bfloat16)

        def one(group, _):
            queries = act_ref[rows, at(2 * V_COLS + group * LANES, LANES)]
            keys = act_ref[rows, at(2 * V_COLS + Q_COLS + group * LANES, LANES)]
            mask = mask_ref[rows, :]
            grad_q = jnp.zeros((length, LANES), jnp.float32)
            grad_k = jnp.zeros((length, LANES), jnp.float32)
            for half in range(GROUP_V // LANES):
                cols = group * GROUP_V + half * LANES
                values = act_ref[rows, at(V_COLS + cols, LANES)]
                grad_mix = dmix[:, at(cols, LANES)]
                grad_v = jnp.zeros((length, LANES), jnp.float32)
                for sub in range(V_HEADS):
                    head = half * V_HEADS + sub
                    mix_head = only_head(grad_mix, lane, V_DIM, sub)
                    place = (slot * HEADS + group * QK_HEADS + head) * length
                    score = score_ref[at(place, length), :]
                    squash = jax.nn.sigmoid(score)
                    weight = (score * squash * mask).astype(jnp.bfloat16)
                    slope = squash * (1.0 + score * (1.0 - squash)) * mask * SCALE
                    grad_score = (dot_nt(mix_head, values) * slope).astype(jnp.bfloat16)
                    grad_v += contract_rows(weight, mix_head)
                    grad_q += dot_nn(grad_score, only_head(keys, lane, QK_DIM, head))
                    grad_k += contract_rows(grad_score, only_head(queries, lane, QK_DIM, head))
                store_grad(rows, V_COLS + cols, LANES, grad_v)
            store_grad(rows, 2 * V_COLS + group * LANES, LANES, grad_q)
            store_grad(rows, 2 * V_COLS + Q_COLS + group * LANES, LANES, grad_k)
            return 0

        lax.fori_loop(0, GROUPS, one, 0)

        def norm_tile(index, _):
            gnorm[:, at(index * tile, tile)] = dot_nt(gpre_ref[rows, :], first_ref[at(index * tile, tile), :])
            return 0

        lax.fori_loop(0, width // tile, norm_tile, 0)
        value = input_ref[rows, :].astype(jnp.float32)
        center = value - jnp.mean(value, axis=-1, keepdims=True)
        rstd = lax.rsqrt(jnp.mean(center * center, axis=-1, keepdims=True) + EPSILON)
        unit = center * rstd
        grad = gnorm[...]
        mean_grad = jnp.mean(grad, axis=-1, keepdims=True)
        mean_unit = jnp.mean(grad * unit, axis=-1, keepdims=True)
        through = rstd * (grad - mean_grad - unit * mean_unit)
        result = (up_ref[rows, :].astype(jnp.float32) + through).astype(jnp.bfloat16)
        leaving[slot] = result
        gin_ref[rows, :] = result

        @pl.when(jnp.logical_not(is_first))
        def _():
            copy_of(slot).start()

    for slot in range(micro):

        @pl.when(jnp.logical_not(is_first))
        def _():
            copy_of(slot).wait_send()


def chain(top, inputs, activated, preact, scores, unit, rstd, mask, w_first, w_second, micro, length):
    tokens, width = inputs.shape
    return pl.pallas_call(
        functools.partial(chain_kernel, micro, length, lax.axis_size("pipe")),
        out_shape=(
            jax.ShapeDtypeStruct((tokens, width), jnp.bfloat16),
            jax.ShapeDtypeStruct(preact.shape, jnp.bfloat16),
            jax.ShapeDtypeStruct((tokens, width), jnp.bfloat16),
        ),
        in_specs=[VMEM] * 10,
        out_specs=(VMEM,) * 3,
        scratch_shapes=[
            pltpu.VMEM((micro, length, width), jnp.bfloat16),
            pltpu.VMEM((micro, length, width), jnp.bfloat16),
            pltpu.VMEM((length, V_COLS), jnp.float32),
            pltpu.VMEM((length, V_COLS), jnp.bfloat16),
            pltpu.VMEM((length, width), jnp.float32),
            pltpu.SemaphoreType.DMA((micro,)),
            pltpu.SemaphoreType.DMA((micro,)),
        ],
        compiler_params=pltpu.CompilerParams(
            collective_id=0, has_side_effects=True, vmem_limit_bytes=60 * 1024 * 1024
        ),
        name="chain",
    )(top, inputs, activated, preact, scores, unit, rstd, mask, w_first, w_second)


def add_into(target, left, right):
    step = 32

    def one(index, _):
        rows = pl.ds(pl.multiple_of(index * step, step), step)
        total = left[rows, :].astype(jnp.float32) + right[rows, :].astype(jnp.float32)
        target[rows, :] = total.astype(target.dtype)
        return 0

    lax.fori_loop(0, target.shape[0] // step, one, 0)


def scatter_kernel(line, part_a, part_b, out_a, out_b, *scratch):
    pairs = (
        (part_a, out_a) + scratch[0:4],
        (part_b, out_b) + scratch[4:8],
    )
    load_sem, pair_send, pair_recv, right_send, right_recv, left_send, left_recv = scratch[8:]
    rank = lax.axis_index("dp")
    spot, lane_of = rank // 2, rank % 2
    has_left, has_right = spot > 0, spot < line - 1
    partner = spot * 2 + 1 - lane_of
    right = jnp.minimum(spot + 1, line - 1) * 2 + lane_of
    left = jnp.maximum(spot - 1, 0) * 2 + lane_of

    barrier = pltpu.get_barrier_semaphore()
    pl.semaphore_signal(barrier, inc=1, device_id={"dp": partner}, device_id_type=MESH)

    @pl.when(has_left)
    def _():
        pl.semaphore_signal(barrier, inc=1, device_id={"dp": left}, device_id_type=MESH)

    @pl.when(has_right)
    def _():
        pl.semaphore_signal(barrier, inc=1, device_id={"dp": right}, device_id_type=MESH)

    pl.semaphore_wait(barrier, 1 + jnp.minimum(spot, 1) + jnp.minimum(line - 1 - spot, 1))

    def block_at(turn):
        near = jnp.minimum(spot, line - 1 - spot)
        ahead = line - 1 - 2 * near
        lone = jnp.where(spot <= line - 1 - spot, line - 1 - turn, turn)
        after = jnp.maximum(turn - ahead, 0)
        reach = near - after // 2
        both = jnp.where(after % 2 == 0, spot + reach, spot - reach)
        return jnp.where(turn < ahead, lone, both)

    def load_of(which, block):
        part, _, own, _, _, _ = pairs[which]
        return pltpu.make_async_copy(part.at[block, lane_of], own.at[block], load_sem.at[which, block])

    def pair_of(which, block):
        part, _, _, paired, _, _ = pairs[which]
        return pltpu.make_async_remote_copy(
            src_ref=part.at[block, 1 - lane_of], dst_ref=paired.at[block],
            send_sem=pair_send.at[which, block], recv_sem=pair_recv.at[which, block],
            device_id={"dp": partner}, device_id_type=MESH,
        )

    def flow_of(which, block, rightward, source):
        flow = pairs[which][4 if rightward else 5]
        sends, recvs = (right_send, right_recv) if rightward else (left_send, left_recv)
        return pltpu.make_async_remote_copy(
            src_ref=source.at[block], dst_ref=flow.at[block],
            send_sem=sends.at[which, block], recv_sem=recvs.at[which, block],
            device_id={"dp": right if rightward else left}, device_id_type=MESH,
        )

    def begin(turn, _):
        block = block_at(turn)
        for which in range(2):
            pair_of(which, block).start()
            load_of(which, block).start()
        return 0

    lax.fori_loop(0, line, begin, 0)

    def pass_on(turn, _):
        block = block_at(turn)
        for which in range(2):
            own, paired = pairs[which][2:4]
            load_of(which, block).wait()
            pair_of(which, block).wait_recv()
            add_into(own.at[block], own.at[block], paired.at[block])
            for rightward in (True, False):
                flow = pairs[which][4 if rightward else 5]
                fed = has_left if rightward else has_right
                wanted = block > spot if rightward else block < spot

                @pl.when(jnp.logical_and(wanted, fed))
                def _():
                    flow_of(which, block, rightward, flow).wait_recv()
                    add_into(flow.at[block], flow.at[block], own.at[block])
                    flow_of(which, block, rightward, flow).start()

                @pl.when(jnp.logical_and(wanted, jnp.logical_not(fed)))
                def _():
                    flow_of(which, block, rightward, own).start()
        return 0

    lax.fori_loop(0, line, pass_on, 0)

    for which in range(2):
        out, own = pairs[which][1:3]
        for rightward in (True, False):
            flow = pairs[which][4 if rightward else 5]

            @pl.when(has_left if rightward else has_right)
            def _():
                flow_of(which, spot, rightward, flow).wait_recv()

        @pl.when(jnp.logical_and(has_left, has_right))
        def _():
            add_into(out, own.at[spot], pairs[which][4].at[spot])
            add_into(out, out, pairs[which][5].at[spot])

        @pl.when(jnp.logical_and(has_left, jnp.logical_not(has_right)))
        def _():
            add_into(out, own.at[spot], pairs[which][4].at[spot])

        @pl.when(jnp.logical_and(has_right, jnp.logical_not(has_left)))
        def _():
            add_into(out, own.at[spot], pairs[which][5].at[spot])

    def finish(block, _):
        for which in range(2):
            pair_of(which, block).wait_send()
            for rightward in (True, False):

                @pl.when(block > spot if rightward else block < spot)
                def _():
                    flow_of(which, block, rightward, pairs[which][2]).wait_send()
        return 0

    lax.fori_loop(0, line, finish, 0)


def scatter_sums(part_a, part_b):
    devices = lax.axis_size("dp")
    line = devices // 2
    parts = [part.reshape(line, 2, part.shape[0] // devices, part.shape[1]) for part in (part_a, part_b)]
    scratch = []
    for part in parts:
        scratch += [pltpu.VMEM((line,) + part.shape[2:], part.dtype)] * 4
    scratch += [pltpu.SemaphoreType.DMA((2, line))] * 7
    return pl.pallas_call(
        functools.partial(scatter_kernel, line),
        out_shape=tuple(jax.ShapeDtypeStruct(part.shape[2:], jnp.float32) for part in parts),
        in_specs=[pl.BlockSpec(memory_space=pl.ANY)] * 2,
        out_specs=(VMEM,) * 2,
        scratch_shapes=scratch,
        compiler_params=pltpu.CompilerParams(
            collective_id=1, has_side_effects=True, vmem_limit_bytes=60 * 1024 * 1024
        ),
        name="scatter_sums",
    )(*parts)


def mask_of(segments):
    length = segments.shape[1]
    same = segments[:, :, None] == segments[:, None, :]
    positions = lax.broadcasted_iota(jnp.int32, (length, length), 0)
    columns = lax.broadcasted_iota(jnp.int32, (length, length), 1)
    counts = jnp.sum(same.astype(jnp.float32), axis=2, keepdims=True)
    allowed = jnp.logical_and(same, (columns <= positions)[None])
    return (allowed.astype(jnp.float32) / counts).reshape(-1, length)


def body(section_input, top_grad, w_in, w_out, segments):
    micro, length = segments.shape
    inputs = section_input[0]
    w_first = lax.all_gather(w_in[0], "dp", axis=0, tiled=True)
    w_mine, w_first = lax.optimization_barrier((w_out[0], w_first))
    w_second = lax.all_gather(w_mine, "dp", axis=0, tiled=True)
    mask = mask_of(segments)
    normed = norm_rows(inputs.astype(jnp.float32)).astype(jnp.bfloat16)
    preact = jnp.dot(normed, w_first, preferred_element_type=jnp.float32)
    activated = jax.nn.silu(preact).astype(jnp.bfloat16)
    scores, unit, rstd, gated = attend(activated, mask, micro, length)
    upstream, grad_preact, grads = chain(
        top_grad, inputs, activated, preact, scores, unit, rstd, mask, w_first, w_second, micro, length
    )
    part_out = contract_rows(gated, upstream).astype(jnp.bfloat16)
    part_in = contract_rows(normed, grad_preact).astype(jnp.bfloat16)
    grad_first, grad_out = scatter_sums(part_in, part_out)
    return (grads[None], grad_first[None], grad_out[None])


def solution(mesh):
    return jax.shard_map(
        body,
        mesh=mesh,
        in_specs=(
            P("pipe", "dp", None),
            P("dp", None),
            P("pipe", "dp", None),
            P("pipe", "dp", None),
            P("dp", None),
        ),
        out_specs=(P("pipe", "dp", None), P("pipe", "dp", None), P("pipe", "dp", None)),
        check_vma=False,
    )
```
